128 devices in a mesh: req: 32 (over z, y, core), head: 4 (over x).
Axes of the slice: x: 4, y: 4, z: 4, core: 2. Of those that a mesh axis runs over, the one named last changes fastest.
Arguments:
- tokens: bfloat16 [128, 64, 2048], P(('req', 'head')), may hold values from -3 to 3
- live: int32 [128, 64], P(('req', 'head')), may hold values from 0 to 1, as said below
- parents: int32 [128, 64], P('req'), may hold values from -1 to 62, as said below
- lengths: int32 [128], P('req'), may hold values from 1 to 2048, as said below
- accepted: int32 [128, 8], P('req'), may hold values from 0 to 31, as said below
- routes: int32 [128, 64, 6], P(('req', 'head')), may hold values from 0 to 63, all different within a row; in each aligned block of 64 rows (0 to 63, 64 to 127, ..., all dimensions but the last counted through in order) at most 8 rows name the same one
- cache: bfloat16 [128, 4, 2048, 256], P('req', 'head'), may hold values from -160 to 160, as said below
- attn_gain: float32 [2048], replicated, may hold values from 0.1 to 1.9
- w_qkv: bfloat16 [2048, 3072], P(None, 'head'), may hold values from -0.125 to 0.125
- w_out: bfloat16 [2048, 2048], P('head'), may hold values from -0.125 to 0.125
- ffn_gain: float32 [2048], replicated, may hold values from 0.1 to 1.9
- shared_gate: bfloat16 [2048, 1408], P(None, 'head'), may hold values from -0.125 to 0.125
- shared_up: bfloat16 [2048, 1408], P(None, 'head'), may hold values from -0.125 to 0.125
- shared_down: bfloat16 [1408, 2048], P('head'), may hold values from -0.15625 to 0.15625
- router: bfloat16 [2048, 64], replicated, may hold values from -0.125 to 0.125
- expert_in: bfloat16 [128, 2048, 1408], P(('req', 'head')), may hold values from -0.125 to 0.125
- expert_out: bfloat16 [128, 704, 2048], P(('req', 'head')), may hold values from -0.21875 to 0.21875
Outputs:
- hidden_out: bfloat16 [128, 64, 2048], P(('req', 'head'))
- accepted_kv: bfloat16 [128, 4, 8, 256], P('req', 'head')
The draws below stay inside these ranges and needn't reach their ends.
Inputs may be any that keep to these rules, and one draw needn't show every extreme that they name: lengths run from 1 to 2048; every draw has a request with all 2048 slots filled. Each request's live entries are its first ones; at least 32 are live and some request has all 64 live. parents[r, 0] = -1 and parents[r, i] < i for i > 0. `accepted`: each request's entries are distinct, ascending, begin with 0 and name live nodes; some request names node 31. `routes`: within the 64 nodes of one request no expert is named more than 8 times, and in some request one expert is named exactly 8 times; the 6 experts of a node differ. `cache`: entries are finite.
All inputs are finite; a program needn't handle non-finite values.
Results may differ from the reference program's by a relative error of at most 0.012.
The reference program's roundings to bfloat16 on the way count: a program that leaves them out, or rounds other values in their place, can miss the bound.
Values may be sent and summed in bfloat16 or wider, within the bound.
A program may use at most 128 MiB of HBM per device.

```python
import math
import jax
import jax.numpy as jnp
import numpy as np
from jax import lax

D = 2048
HEADS = 16
KVH = 4
HD = 128
EXP_FF = 1408
TOP = 6
SHARED_FF = 1408
CACHE = 2048
TREE = 64
ACCEPT = 8
REQS = 128
EXPERTS = 64
CAP = 8


def draw_live(key, part):
    key_count, key_full = jax.random.split(key, 2)
    counts = jax.random.randint(key_count, (REQS,), TREE // 2, TREE + 1)
    full_one = jax.random.randint(key_full, (), 0, REQS)
    counts = jnp.where(jnp.arange(REQS) == full_one, TREE, counts)
    return (jnp.arange(TREE)[None, :] < counts[:, None]).astype(jnp.int32)


def draw_parents(key, part):
    nodes = jnp.arange(TREE, dtype=jnp.int32)
    lower = jnp.maximum(nodes - 6, 0)
    upper = jnp.maximum(nodes, 1)
    picked = jax.random.randint(key, (REQS, TREE), lower[None, :], upper[None, :])
    return jnp.where(nodes[None, :] == 0, -1, picked).astype(jnp.int32)


def draw_lengths(key, part):
    key_shift, key_len, key_full = jax.random.split(key, 3)
    shrink = jax.random.randint(key_shift, (REQS,), 0, 6)
    base = CACHE // jnp.power(2, shrink)
    picked = jax.random.randint(key_len, (REQS,), base // 2 + 1, base + 1)
    full_one = jax.random.randint(key_full, (), 0, REQS)
    return jnp.where(jnp.arange(REQS) == full_one, CACHE, picked).astype(jnp.int32)


def draw_accepted(key, part):
    key_rows, key_full = jax.random.split(key, 2)
    row_keys = jax.random.split(key_rows, REQS)

    def one_row(row_key):
        order = jax.random.permutation(row_key, TREE // 2 - 1) + 1
        return jnp.sort(order[:ACCEPT - 1])
    rest = jax.vmap(one_row)(row_keys)
    full_one = jax.random.randint(key_full, (), 0, REQS)
    rest = rest.at[full_one, ACCEPT - 2].set(TREE // 2 - 1)
    return jnp.concatenate([jnp.zeros((REQS, 1), jnp.int32), rest.astype(jnp.int32)], axis=1)


def draw_cache(key, part):
    key_keys, key_values = jax.random.split(key, 2)
    shape = (REQS, KVH, CACHE, HD)
    keys = jnp.clip(jax.random.normal(key_keys, shape, jnp.float32), -6.0, 6.0)
    values = jnp.clip(6.0 * jax.random.normal(key_values, shape, jnp.float32), -36.0, 36.0)
    return jnp.concatenate([keys, values], axis=-1).astype(jnp.bfloat16)


def levels(rng, shape, cuts, least, largest):
    loudness, own = 1.0, jax.random.fold_in(rng, 6)
    for dim, blocks in cuts:
        draws = jnp.exp(jax.random.uniform(jax.random.fold_in(own, dim), (blocks,), jnp.float32, least / len(cuts), largest / len(cuts)))
        loudness = loudness * jnp.repeat(draws, shape[dim] // blocks).reshape([-1 if axis == dim else 1 for axis in range(len(shape))])
    return loudness


def assign_block(rng, own, number, rows, number_of, top, most, slope):
    ranking = jax.random.permutation(rng, number_of)
    packed, usual = shares(number_of, rows * top, most, slope, True), shares(number_of, rows * top, most, slope, False)
    places = jnp.arange(number_of)

    def named(sizes, rotation):
        used = int((sizes > 0).sum())
        fixed = max(1, used // 4)
        moved = fixed + (places - fixed + rotation * (used - fixed)) % max(1, number_of - fixed)
        return jnp.zeros((number_of,), jnp.int32).at[ranking[jnp.where(places < fixed, places, moved)]].set(jnp.asarray(sizes, jnp.int32))

    sizes = jnp.where(number % 4 == 0, named(packed, number // 4), named(usual, number - number // 4 - 1))
    mixed = jax.random.permutation(jax.random.fold_in(own, 3), number_of)
    donor, sink = mixed[0:number_of // 2 * 2:2], mixed[1:number_of // 2 * 2:2]
    slack = jnp.minimum(sizes[donor] - 1, most - sizes[sink]) // 2
    slack = jnp.where((donor == ranking[0]) | (sink == ranking[0]) | (sizes[sink] == 0), 0, jnp.maximum(slack, 0))
    moved = jax.random.randint(jax.random.fold_in(own, 4), (number_of // 2,), 0, 1 << 20) % (slack + 1)
    sizes = sizes.at[donor].add(-moved).at[sink].add(moved)
    items = jnp.searchsorted(jnp.cumsum(sizes), jnp.arange(rows * top), side="right").astype(jnp.int32)
    listing = items.reshape(top, rows).T
    listing = listing[jax.random.permutation(jax.random.fold_in(own, 1), rows)]
    rotation = jax.random.randint(jax.random.fold_in(own, 2), (rows, 1), 0, top)
    return jnp.take_along_axis(listing, (jnp.arange(top)[None, :] + rotation) % top, axis=1)


def shares(count, total, bound, skew, full):
    loads = [(1 << 20) // math.isqrt(standing ** skew) + 1 for standing in range(1, count + 1)]
    largest = bound if full else min(bound, max(-(-total // count), total * loads[0] // sum(loads)))
    least = 1 if total - largest >= count - 1 else 0
    given, surplus = [largest] + [least] * (count - 1), total - largest - least * (count - 1)
    while surplus > 0:
        movable = [i for i in range(1, count) if given[i] < largest] or [i for i in range(1, count) if given[i] < bound]
        mass, left = sum([loads[i] for i in movable]), surplus
        for i in movable:
            addition = min(bound - given[i], max(1, left * loads[i] // mass), surplus)
            given[i] = given[i] + addition
            surplus = surplus - addition
    return np.array(given)


def centred(stream_key, extent, scale, bound, cuts=(), kind=jnp.bfloat16):
    factor_of = levels(stream_key, extent, cuts, -0.22, 0.18) if cuts else 1.0
    drawn = jax.random.normal(stream_key, extent, jnp.float32) * scale * factor_of
    return jnp.minimum(jnp.maximum(drawn, -bound), bound).astype(kind)


def setup_inputs(seed: int = 0) -> dict:
    key_list = jax.random.split(jax.random.key(seed), 18)
    tokens = centred(key_list[0], (REQS, TREE, D), 0.5, 3.0, ((0, 128),))
    live = draw_live(jax.random.fold_in(key_list[17], 71), 0)
    parents = draw_parents(jax.random.fold_in(key_list[17], 71), 0)
    lengths = draw_lengths(jax.random.fold_in(key_list[17], 71), 0)
    accepted = draw_accepted(jax.random.fold_in(key_list[17], 71), 0)
    routes_keys = jax.random.split(jax.random.fold_in(key_list[5], 1), REQS * TREE // TREE)
    routes_turns = jax.random.permutation(jax.random.fold_in(key_list[5], 3), REQS * TREE // TREE)
    routes = jax.vmap(lambda own, number: assign_block(jax.random.fold_in(key_list[5], 2), own, number, TREE, EXPERTS, TOP, CAP, 2))(routes_keys, routes_turns).reshape((REQS, TREE, TOP))
    cache = draw_cache(jax.random.fold_in(key_list[17], 71), 0)
    attn_gain = jnp.clip(1.0 + 0.18 * jax.random.normal(key_list[7], (D,), jnp.float32), 0.1, 1.9)
    w_qkv = centred(key_list[8], (D, KVH * (HEADS // KVH + 2) * HD), D ** -0.5, 0.125, ((1, 4),))
    w_out = centred(key_list[9], (HEADS * HD, D), (HEADS * HD) ** -0.5, 0.125, ((0, 4),))
    ffn_gain = jnp.clip(1.0 + 0.18 * jax.random.normal(key_list[10], (D,), jnp.float32), 0.1, 1.9)
    shared_gate = centred(key_list[11], (D, SHARED_FF), D ** -0.5, 0.125, ((1, 4),))
    shared_up = centred(key_list[12], (D, SHARED_FF), D ** -0.5, 0.125, ((1, 4),))
    shared_down = centred(key_list[13], (SHARED_FF, D), SHARED_FF ** -0.5, 0.15625, ((0, 4),))
    router = centred(key_list[14], (D, EXPERTS), D ** -0.5, 0.125)
    expert_in = centred(key_list[15], (2 * EXPERTS, D, EXP_FF), D ** -0.5, 0.125, ((0, 128),))
    expert_out = centred(key_list[16], (2 * EXPERTS, EXP_FF // 2, D), (EXP_FF // 2) ** -0.5, 0.21875, ((0, 128),))
    return {"tokens": tokens, "live": live, "parents": parents, "lengths": lengths, "accepted": accepted, "routes": routes, "cache": cache, "attn_gain": attn_gain, "w_qkv": w_qkv, "w_out": w_out, "ffn_gain": ffn_gain, "shared_gate": shared_gate, "shared_up": shared_up, "shared_down": shared_down, "router": router, "expert_in": expert_in, "expert_out": expert_out}


EPSILON = 1e-06
ROPE_BASE = 10000.0

def rms_norm(values, gain):
    wide = values.astype(jnp.float32)
    power = lax.optimization_barrier(jnp.mean(wide * wide, axis=-1, keepdims=True))
    return (wide * lax.rsqrt(power + EPSILON) * gain).astype(jnp.bfloat16)

def rotate(values, position):
    half = values.shape[-1] // 2
    frequency = ROPE_BASE ** (-jnp.arange(half, dtype=jnp.float32) / half)
    angle = position[..., None] * frequency
    cosine = jnp.cos(angle)
    sine = jnp.sin(angle)
    first = values[..., :half]
    second = values[..., half:]
    return jnp.concatenate([first * cosine - second * sine, second * cosine + first * sine], axis=-1)

def ancestry(parents):
    nodes_count = parents.shape[-1]
    nodes = jnp.arange(nodes_count, dtype=jnp.int32)
    reach = (parents[..., :, None] == nodes).astype(jnp.float32) + jnp.eye(nodes_count, dtype=jnp.float32)
    for turn in range(nodes_count.bit_length()):
        reach = jnp.minimum(jnp.einsum('rij,rjk->rik', reach, reach, precision=lax.Precision.HIGHEST), 1.0)
    depth = lax.optimization_barrier(jnp.sum(reach, axis=-1)) - 1.0
    return (reach, depth)

def head_group(projected, position, length, reach, cache_rows):
    group = projected.shape[0] - 2
    tree = projected.shape[1]
    head_dim = projected.shape[2]
    query = rotate(projected[:group], position).astype(jnp.bfloat16).reshape(group * tree, head_dim)
    key_new = rotate(projected[group], position).astype(jnp.bfloat16)
    value_new = projected[group + 1].astype(jnp.bfloat16)
    scale = 1.0 / math.sqrt(head_dim)
    cache_keys = cache_rows[:, :head_dim]
    cache_values = cache_rows[:, head_dim:]
    old_scores = jnp.einsum('qd,kd->qk', query, cache_keys, preferred_element_type=jnp.float32) * scale
    new_scores = jnp.einsum('qd,kd->qk', query, key_new, preferred_element_type=jnp.float32) * scale
    visible = jnp.arange(cache_rows.shape[0], dtype=jnp.int32) < length
    old_scores = jnp.where(visible[None, :], old_scores, -1e+30)
    new_scores = jnp.where(jnp.tile(reach, (group, 1)) > 0.5, new_scores, -1e+30)
    peak = jnp.maximum(lax.optimization_barrier(jnp.max(old_scores, axis=-1, keepdims=True)), lax.optimization_barrier(jnp.max(new_scores, axis=-1, keepdims=True)))
    old_weights = jnp.exp(old_scores - peak)
    new_weights = jnp.exp(new_scores - peak)
    denominator = lax.optimization_barrier(jnp.sum(old_weights, axis=-1, keepdims=True)) + lax.optimization_barrier(jnp.sum(new_weights, axis=-1, keepdims=True))
    old_probs = (old_weights / denominator).astype(jnp.bfloat16)
    new_probs = (new_weights / denominator).astype(jnp.bfloat16)
    mixed = jnp.dot(old_probs, cache_values, preferred_element_type=jnp.float32) + jnp.dot(new_probs, value_new, preferred_element_type=jnp.float32)
    mixed = mixed.astype(jnp.bfloat16).reshape(group, tree, head_dim).transpose(1, 0, 2).reshape(tree, group * head_dim)
    return (mixed, jnp.concatenate([key_new, value_new], axis=-1))

def expert_half(rows, inner, outer):
    both = jnp.dot(rows, inner, preferred_element_type=jnp.float32)
    half = inner.shape[1] // 2
    hidden = (jax.nn.silu(both[:, :half]) * both[:, half:]).astype(jnp.bfloat16)
    return jnp.dot(hidden, outer, preferred_element_type=jnp.float32).astype(jnp.bfloat16)

def reference(tokens, live, parents, lengths, accepted, routes, cache, attn_gain, w_qkv, w_out, ffn_gain, shared_gate, shared_up, shared_down, router, expert_in, expert_out):
    request_count, tree, width = tokens.shape
    kv_heads = cache.shape[1]
    head_dim = cache.shape[3] // 2
    group = w_qkv.shape[1] // (kv_heads * head_dim) - 2
    top_count = routes.shape[2]
    expert_count = router.shape[1]
    capacity = 4 * tree * top_count // (3 * expert_count)
    normed = rms_norm(tokens, attn_gain)
    reach, depth = ancestry(parents)
    positions = lengths[:, None].astype(jnp.float32) + depth

    def one_request(inputs):
        rows, raw_rows, reach_one, position, length, chosen, cache_one = inputs
        projected = jnp.dot(rows, w_qkv, preferred_element_type=jnp.float32)
        projected = projected.reshape(tree, kv_heads, group + 2, head_dim).transpose(1, 2, 0, 3)
        mixed, fresh = jax.vmap(head_group, in_axes=(0, None, None, None, 0))(projected, position, length, reach_one, cache_one)
        mixed = mixed.transpose(1, 0, 2).reshape(tree, kv_heads * group * head_dim)
        attn = jnp.dot(mixed, w_out, preferred_element_type=jnp.float32)
        resid_one = (raw_rows.astype(jnp.float32) + attn).astype(jnp.bfloat16)
        return (resid_one, fresh[:, chosen])
    resid, accepted_kv = lax.map(one_request, (normed, tokens, reach, positions, lengths, accepted, cache))
    normed2 = rms_norm(resid, ffn_gain)
    flat = normed2.reshape(request_count * tree, width)
    shared_hidden = (jax.nn.silu(jnp.dot(flat, shared_gate, preferred_element_type=jnp.float32)) * jnp.dot(flat, shared_up, preferred_element_type=jnp.float32)).astype(jnp.bfloat16)
    shared = jnp.dot(shared_hidden, shared_down, preferred_element_type=jnp.float32)
    logits = jnp.dot(flat, router, preferred_element_type=jnp.float32)
    route_flat = routes.reshape(request_count * tree, top_count)
    picked = jax.nn.sigmoid(jnp.take_along_axis(logits, route_flat, axis=1))
    gates = picked / lax.optimization_barrier(jnp.sum(picked, axis=-1, keepdims=True))
    assign = routes.reshape(request_count, tree * top_count)
    onehot = (assign[..., None] == jnp.arange(expert_count, dtype=jnp.int32)).astype(jnp.int32)
    earlier = jnp.cumsum(onehot, axis=1) - onehot
    slots = lax.optimization_barrier(jnp.sum(earlier * onehot, axis=-1)).astype(jnp.int32)
    request_rows = jnp.broadcast_to(jnp.arange(request_count, dtype=jnp.int32)[:, None], assign.shape)
    token_ids = (jnp.arange(request_count * tree * top_count, dtype=jnp.int32) // top_count).reshape(request_count, tree * top_count)
    table = jnp.zeros((expert_count, request_count, capacity), jnp.int32).at[assign, request_rows, slots].set(token_ids)
    gate_table = jnp.zeros((expert_count, request_count, capacity), jnp.float32).at[assign, request_rows, slots].set(gates.reshape(request_count, tree * top_count))
    inner_all = expert_in.reshape(expert_count, 2, width, expert_in.shape[2])
    outer_all = expert_out.reshape(expert_count, 2, expert_out.shape[1], width)

    def one_expert(total, inputs):
        rows_index, rows_gate, inner, outer = inputs
        index_flat = rows_index.reshape(-1)
        chosen_rows = flat[index_flat]
        first = expert_half(chosen_rows, inner[0], outer[0]).astype(jnp.float32)
        second = expert_half(chosen_rows, inner[1], outer[1]).astype(jnp.float32)
        total = total.at[index_flat].add(rows_gate.reshape(-1, 1) * (first + second))
        return (total, None)
    routed, unused = lax.scan(one_expert, jnp.zeros((request_count * tree, width), jnp.float32), (table, gate_table, inner_all, outer_all))
    total_out = resid.reshape(request_count * tree, width).astype(jnp.float32) + shared + routed
    keep = live.reshape(request_count * tree, 1) == 1
    hidden_out = jnp.where(keep, total_out, 0.0).astype(jnp.bfloat16).reshape(request_count, tree, width)
    return (hidden_out, accepted_kv)
```

```python
import functools
import math

import jax
import jax.numpy as jnp
from jax import lax
from jax.experimental import pallas as pl
from jax.experimental.pallas import tpu as pltpu
from jax.sharding import PartitionSpec as P

EPSILON = 1e-06
ROPE_BASE = 10000.0
MESH = pl.DeviceIdType.MESH
NX, NY, NZ, NC = 4, 4, 4, 2
GROUP = NY * NZ * NC
VMEM = pl.BlockSpec(memory_space=pltpu.VMEM)


def rms_norm(values, gain):
    wide = values.astype(jnp.float32)
    power = jnp.mean(wide * wide, axis=-1, keepdims=True)
    return (wide * lax.rsqrt(power + EPSILON) * gain).astype(jnp.bfloat16)


def rotate(values, position):
    half = values.shape[-1] // 2
    frequency = ROPE_BASE ** (-jnp.arange(half, dtype=jnp.float32) / half)
    angle = position[..., None] * frequency
    cosine = jnp.cos(angle)
    sine = jnp.sin(angle)
    first = values[..., :half]
    second = values[..., half:]
    return jnp.concatenate(
        [first * cosine - second * sine, second * cosine + first * sine], axis=-1
    )


def ancestry(parents):
    nodes_count = parents.shape[-1]
    nodes = jnp.arange(nodes_count, dtype=jnp.int32)
    reach = (parents[..., :, None] == nodes).astype(jnp.bfloat16) + jnp.eye(
        nodes_count, dtype=jnp.bfloat16
    )
    for turn in range((nodes_count - 1).bit_length()):
        reach = jnp.minimum(
            jnp.einsum("rij,rjk->rik", reach, reach, preferred_element_type=jnp.float32), 1.0
        ).astype(jnp.bfloat16)
    reach = reach.astype(jnp.float32)
    depth = jnp.sum(reach, axis=-1) - 1.0
    return (reach, depth)


def head_group(projected, position, length, reach, cache_rows):
    group = projected.shape[0] - 2
    tree = projected.shape[1]
    head_dim = projected.shape[2]
    query = rotate(projected[:group], position).astype(jnp.bfloat16).reshape(group * tree, head_dim)
    key_new = rotate(projected[group], position).astype(jnp.bfloat16)
    value_new = projected[group + 1].astype(jnp.bfloat16)
    scale = 1.0 / math.sqrt(head_dim)
    cache_keys = cache_rows[:, :head_dim]
    cache_values = cache_rows[:, head_dim:]
    old_scores = (
        jnp.einsum("qd,kd->qk", query, cache_keys, preferred_element_type=jnp.float32) * scale
    )
    new_scores = jnp.einsum("qd,kd->qk", query, key_new, preferred_element_type=jnp.float32) * scale
    visible = jnp.arange(cache_rows.shape[0], dtype=jnp.int32) < length
    old_scores = jnp.where(visible[None, :], old_scores, -1e30)
    new_scores = jnp.where(jnp.tile(reach, (group, 1)) > 0.5, new_scores, -1e30)
    peak = jnp.maximum(
        jnp.max(old_scores, axis=-1, keepdims=True), jnp.max(new_scores, axis=-1, keepdims=True)
    )
    old_weights = jnp.exp(old_scores - peak)
    new_weights = jnp.exp(new_scores - peak)
    denominator = jnp.sum(old_weights, axis=-1, keepdims=True) + jnp.sum(
        new_weights, axis=-1, keepdims=True
    )
    old_probs = (old_weights / denominator).astype(jnp.bfloat16)
    new_probs = (new_weights / denominator).astype(jnp.bfloat16)
    mixed = jnp.dot(old_probs, cache_values, preferred_element_type=jnp.float32) + jnp.dot(
        new_probs, value_new, preferred_element_type=jnp.float32
    )
    mixed = (
        mixed.astype(jnp.bfloat16)
        .reshape(group, tree, head_dim)
        .transpose(1, 0, 2)
        .reshape(tree, group * head_dim)
    )
    return (mixed, jnp.concatenate([key_new, value_new], axis=-1))


def place():
    r = lax.axis_index("req")
    return r // (NY * NC), (r // NC) % NY, r % NC, lax.axis_index("head")


def device(z, y, c, x):
    return (z * (NY * NC) + y * NC + c, x)


def rendezvous(peers):
    barrier = pltpu.get_barrier_semaphore()
    for peer in peers:
        pl.semaphore_signal(barrier, inc=1, device_id=peer, device_id_type=MESH)
    pl.semaphore_wait(barrier, len(peers))


def remote(src, dst, send, recv, peer):
    return pltpu.make_async_remote_copy(
        src_ref=src, dst_ref=dst, send_sem=send, recv_sem=recv, device_id=peer, device_id_type=MESH
    )


def gather_kernel(rows_ref, table_ref, rows_out, table_out, send, recv, local):
    z, y, c, x = place()
    peers = [device(z, y, c, (x + d) % NX) for d in (1, 3, 2)]
    rendezvous(peers)
    copies = []
    for i, peer in enumerate(peers):
        copies.append(remote(table_ref, table_out.at[x], send.at[1, i], recv.at[1, i], peer))
        copies.append(remote(rows_ref, rows_out.at[x], send.at[0, i], recv.at[0, i], peer))
    for copy in copies:
        copy.start()
    own = [
        pltpu.make_async_copy(rows_ref, rows_out.at[x], local.at[0]),
        pltpu.make_async_copy(table_ref, table_out.at[x], local.at[1]),
    ]
    for copy in own:
        copy.start()
    for copy in own + copies:
        copy.wait()


def gather_rows(rows, table):
    return pl.pallas_call(
        gather_kernel,
        out_shape=(
            jax.ShapeDtypeStruct((NX,) + rows.shape, rows.dtype),
            jax.ShapeDtypeStruct((NX,) + table.shape, table.dtype),
        ),
        in_specs=[VMEM, VMEM],
        out_specs=(VMEM, VMEM),
        scratch_shapes=[
            pltpu.SemaphoreType.DMA((2, 3)),
            pltpu.SemaphoreType.DMA((2, 3)),
            pltpu.SemaphoreType.DMA((2,)),
        ],
        compiler_params=pltpu.CompilerParams(collective_id=1, has_side_effects=True),
        name="gather_rows",
    )(rows, table)


PIECES = 2


def resid_kernel(term_ref, own_ref, gain_ref, resid_out, normed_out, got, mine, send, recv, send2, recv2):
    z, y, c, x = place()
    peers = [(x + d) % NX for d in (1, 3, 2)]
    rendezvous([device(z, y, c, p) for p in peers])
    rows = own_ref.shape[0] // PIECES
    first = []
    for piece in range(PIECES):
        part = pl.ds(piece * rows, rows)
        for i, p in enumerate(peers):
            copy = remote(
                term_ref.at[p, part], got.at[i, part], send.at[piece, i], recv.at[piece, i],
                device(z, y, c, p),
            )
            copy.start()
            first.append(copy)
    second = []
    for piece in range(PIECES):
        part = pl.ds(piece * rows, rows)
        for i in range(3):
            first[piece * 3 + i].wait_recv()
        total = own_ref[part]
        for i in range(3):
            total = total + got[i, part].astype(jnp.float32)
        resid = total.astype(jnp.bfloat16)
        resid_out[part] = resid
        normed = rms_norm(resid, gain_ref[...])
        mine[part] = normed
        normed_out[x, part] = normed
        for i, p in enumerate(peers):
            copy = remote(
                mine.at[part], normed_out.at[x, part], send2.at[piece, i], recv2.at[piece, i],
                device(z, y, c, p),
            )
            copy.start()
            second.append(copy)
    for copy in first:
        copy.wait_send()
    for copy in second:
        copy.wait()


def resid_rows(term, own, gain):
    rows, width = own.shape
    sem = pltpu.SemaphoreType.DMA((PIECES, 3))
    return pl.pallas_call(
        resid_kernel,
        out_shape=(
            jax.ShapeDtypeStruct((rows, width), jnp.bfloat16),
            jax.ShapeDtypeStruct((NX, rows, width), jnp.bfloat16),
        ),
        in_specs=[VMEM] * 3,
        out_specs=(VMEM, VMEM),
        scratch_shapes=[
            pltpu.VMEM((3, rows, width), jnp.bfloat16),
            pltpu.VMEM((rows, width), jnp.bfloat16),
            sem, sem, sem, sem,
        ],
        compiler_params=pltpu.CompilerParams(collective_id=2, has_side_effects=True),
        name="resid_rows",
    )(term, own, gain)


def exchange_kernel(src, out, mid_y, mid_z, send1, recv1, send2, recv2, local):
    z, y, c, x = place()
    half = src.shape[-1] // 2
    left, right = pl.ds(0, half), pl.ds(half, half)
    order = (1, 3, 2)
    peers = [device(z, (y + d) % NY, (c + e) % NC, x) for d in order for e in range(NC)]
    peers += [device((z + d) % NZ, y, (c + e) % NC, x) for d in order for e in range(NC)]
    peers += [device(z, y, 1 - c, x)]
    rendezvous(peers)
    copies = []
    arrive_y, arrive_z = {}, {}
    for d in order:
        yd, zd = (y + d) % NY, (z + d) % NZ
        copy = remote(
            src.at[:, yd, :, :, left], mid_y.at[d - 1], send1.at[0, d - 1], recv1.at[0, d - 1],
            device(z, yd, c, x),
        )
        copy.start()
        arrive_y[d] = copy
        copy = remote(
            src.at[zd, :, :, :, right], mid_z.at[d - 1], send1.at[1, d - 1], recv1.at[1, d - 1],
            device(zd, y, c, x),
        )
        copy.start()
        arrive_z[d] = copy

    for d in (0,) + order:
        ys, zs = (y - d) % NY, (z - d) % NZ
        if d:
            arrive_y[d].wait_recv()
            arrive_z[d].wait_recv()
        for f in order + (0,):
            yf, zf = (y + f) % NY, (z + f) % NZ
            for e in range(NC):
                ce = (c + e) % NC
                slot = (d * 4 + f) * NC + e
                a = src.at[zf, y, ce, :, left] if d == 0 else mid_y.at[d - 1, zf, ce]
                b = src.at[z, yf, ce, :, right] if d == 0 else mid_z.at[d - 1, yf, ce]
                to_a, to_b = out.at[z, ys, c, :, left], out.at[zs, y, c, :, right]
                if f == 0 and e == 0:
                    pair = [
                        pltpu.make_async_copy(a, to_a, local.at[0, d]),
                        pltpu.make_async_copy(b, to_b, local.at[1, d]),
                    ]
                else:
                    pair = [
                        remote(a, to_a, send2.at[0, slot], recv2.at[0, slot], device(zf, y, ce, x)),
                        remote(b, to_b, send2.at[1, slot], recv2.at[1, slot], device(z, yf, ce, x)),
                    ]
                for copy in pair:
                    copy.start()
                copies += pair
    for d in order:
        arrive_y[d].wait_send()
        arrive_z[d].wait_send()
    for copy in copies:
        copy.wait()


def exchange(blocks, identifier):
    rows, width = blocks.shape[-2:]
    return pl.pallas_call(
        exchange_kernel,
        out_shape=jax.ShapeDtypeStruct(blocks.shape, blocks.dtype),
        in_specs=[VMEM],
        out_specs=VMEM,
        scratch_shapes=[
            pltpu.VMEM((3, NZ, NC, rows, width // 2), blocks.dtype),
            pltpu.VMEM((3, NY, NC, rows, width // 2), blocks.dtype),
            pltpu.SemaphoreType.DMA((2, 3)),
            pltpu.SemaphoreType.DMA((2, 3)),
            pltpu.SemaphoreType.DMA((2, 32)),
            pltpu.SemaphoreType.DMA((2, 32)),
            pltpu.SemaphoreType.DMA((2, 4)),
        ],
        compiler_params=pltpu.CompilerParams(collective_id=identifier, has_side_effects=True),
        name="exchange",
    )(blocks)


def final_kernel(part_ref, own_ref, live_ref, out, got, send, recv):
    z, y, c, x = place()
    peers = [(x + d) % NX for d in (1, 3, 2)]
    rendezvous([device(z, y, c, p) for p in peers])
    copies = [
        remote(part_ref.at[p], got.at[i], send.at[i], recv.at[i], device(z, y, c, p))
        for i, p in enumerate(peers)
    ]
    for copy in copies:
        copy.start()
    for copy in copies:
        copy.wait()
    total = own_ref[...]
    for i in range(3):
        total = total + got[i].astype(jnp.float32)
    out[...] = jnp.where(live_ref[...] == 1, total, 0.0).astype(jnp.bfloat16)


def final_rows(part, own, live):
    rows, width = own.shape
    return pl.pallas_call(
        final_kernel,
        out_shape=jax.ShapeDtypeStruct((rows, width), jnp.bfloat16),
        in_specs=[VMEM] * 3,
        out_specs=VMEM,
        scratch_shapes=[
            pltpu.VMEM((3, rows, width), jnp.bfloat16),
            pltpu.SemaphoreType.DMA((3,)),
            pltpu.SemaphoreType.DMA((3,)),
        ],
        compiler_params=pltpu.CompilerParams(collective_id=5, has_side_effects=True),
        name="final_rows",
    )(part, own, live)


def expert_half(rows, inner, outer):
    both = jnp.dot(rows, inner, preferred_element_type=jnp.float32)
    half = inner.shape[1] // 2
    hidden = (jax.nn.silu(both[:, :half]) * both[:, half:]).astype(jnp.bfloat16)
    return jnp.dot(hidden, outer, preferred_element_type=jnp.float32).astype(jnp.bfloat16)


def body(
    tokens,
    live,
    parents,
    lengths,
    accepted,
    routes,
    cache,
    attn_gain,
    w_qkv,
    w_out,
    ffn_gain,
    shared_gate,
    shared_up,
    shared_down,
    router,
    expert_in,
    expert_out,
):
    tree, width = tokens.shape[1:]
    own_rows = tokens[0]
    x = lax.axis_index("head")
    local_heads = cache.shape[1]
    head_dim = cache.shape[3] // 2
    group = w_qkv.shape[1] // (local_heads * head_dim) - 2
    top_count = routes.shape[2]
    expert_count = router.shape[1]
    capacity = 4 * tree * top_count // (3 * expert_count)

    table = jnp.pad(routes[0].T, ((0, 8 - top_count), (0, 128 - tree)))
    normed_all, table_all = gather_rows(rms_norm(own_rows, attn_gain), table)

    projected = jnp.dot(
        normed_all.reshape(NX * tree, width), w_qkv, preferred_element_type=jnp.float32
    )
    projected = projected.reshape(NX, tree, local_heads, group + 2, head_dim).transpose(
        0, 2, 3, 1, 4
    )
    reach, depth = ancestry(parents)
    positions = lengths[:, None].astype(jnp.float32) + depth
    inner_map = jax.vmap(head_group, in_axes=(0, None, None, None, 0))
    mixed, fresh = jax.vmap(inner_map)(projected, positions, lengths, reach, cache)
    mixed = mixed.transpose(0, 2, 1, 3).reshape(NX * tree, local_heads * group * head_dim)
    accepted_kv = jnp.take_along_axis(fresh, accepted[:, None, :, None], axis=2)

    term = jnp.dot(mixed, w_out, preferred_element_type=jnp.float32).reshape(NX, tree, width)
    own_term = lax.dynamic_index_in_dim(term, x, 0, keepdims=False) + own_rows.astype(jnp.float32)
    resid, normed2 = resid_rows(term.astype(jnp.bfloat16), own_term, ffn_gain[None])
    normed2 = normed2.reshape(NX * tree, width)

    choose = table_all[:, :top_count, :tree]
    named = jnp.any(
        choose[:, :, :, None] == jnp.arange(expert_count, dtype=jnp.int32), axis=1
    ).astype(jnp.float32)
    earlier = jnp.tril(jnp.ones((tree, tree), jnp.bfloat16), -1)
    rank = jnp.einsum(
        "ts,rse->rte", earlier, named.astype(jnp.bfloat16), preferred_element_type=jnp.float32
    )
    logits = jnp.dot(normed2, router, preferred_element_type=jnp.float32)
    picked = jax.nn.sigmoid(logits).reshape(NX, tree, expert_count) * named
    gates = picked / jnp.sum(picked, axis=-1, keepdims=True)
    pair = x // 2
    slot = jnp.where(named > 0.5, rank, -1.0)

    def of_pair(values):
        values = values.reshape(NX, tree, GROUP, expert_count // GROUP)
        return jnp.where(pair == 0, values[..., 0], values[..., 1])

    slot = of_pair(slot)
    gates = of_pair(gates)
    same = jnp.arange(NX)[:, None, None, None, None] == jnp.arange(NX)[:, None]
    taken = (slot[:, :, :, None, None] == jnp.arange(capacity, dtype=jnp.float32)) & same
    taken = taken.reshape(NX * tree, GROUP * NX * capacity)
    weight = jnp.broadcast_to(
        gates[:, :, :, None, None], (NX, tree, GROUP, NX, capacity)
    ).reshape(NX * tree, GROUP * NX * capacity)
    weight = jnp.where(taken, weight, 0.0)
    weight_high = weight.astype(jnp.bfloat16)
    weight_low = (weight - weight_high.astype(jnp.float32)).astype(jnp.bfloat16)
    outgoing = lax.dot_general(
        taken.astype(jnp.bfloat16), normed2, (((0,), (0,)), ((), ())),
        preferred_element_type=jnp.float32,
    ).astype(jnp.bfloat16)
    blocks = (NZ, NY, NC, NX * capacity, width)
    received = exchange(outgoing.reshape(blocks), 3)
    half_out = expert_half(received.reshape(-1, width), expert_in[0], expert_out[0])
    returned = exchange(half_out.reshape(blocks), 4).reshape(-1, width)

    gated = jax.nn.silu(jnp.dot(normed2, shared_gate, preferred_element_type=jnp.float32))
    hidden = (gated * jnp.dot(normed2, shared_up, preferred_element_type=jnp.float32)).astype(
        jnp.bfloat16
    )
    part = (
        jnp.dot(hidden, shared_down, preferred_element_type=jnp.float32)
        + jnp.dot(weight_high, returned, preferred_element_type=jnp.float32)
        + jnp.dot(weight_low, returned, preferred_element_type=jnp.float32)
    ).reshape(NX, tree, width)
    own_part = lax.dynamic_index_in_dim(part, x, 0, keepdims=False) + resid.astype(jnp.float32)
    hidden_out = final_rows(part.astype(jnp.bfloat16), own_part, live.reshape(tree, 1))
    return (hidden_out[None], accepted_kv)


def solution(mesh):
    in_specs = (
        P(("req", "head"), None, None),
        P(("req", "head"), None),
        P("req", None),
        P("req"),
        P("req", None),
        P(("req", "head"), None, None),
        P("req", "head", None, None),
        P(),
        P(None, "head"),
        P("head", None),
        P(),
        P(None, "head"),
        P(None, "head"),
        P("head", None),
        P(),
        P(("req", "head"), None, None),
        P(("req", "head"), None, None),
    )
    out_specs = (P(("req", "head"), None, None), P("req", "head", None, None))
    return jax.shard_map(body, mesh=mesh, in_specs=in_specs, out_specs=out_specs, check_vma=False)
```

```python
import functools
import math

import jax
import jax.numpy as jnp
from jax import lax
from jax.experimental import pallas as pl
from jax.experimental.pallas import tpu as pltpu
from jax.sharding import PartitionSpec as P

EPSILON = 1e-06
ROPE_BASE = 10000.0
MESH = pl.DeviceIdType.MESH
NX, NY, NZ, NC = 4, 4, 4, 2
GROUP = NY * NZ * NC
VMEM = pl.BlockSpec(memory_space=pltpu.VMEM)


def rms_norm(values, gain):
    wide = values.astype(jnp.float32)
    power = jnp.mean(wide * wide, axis=-1, keepdims=True)
    return (wide * lax.rsqrt(power + EPSILON) * gain).astype(jnp.bfloat16)


def place():
    r = lax.axis_index("req")
    return r // (NY * NC), (r // NC) % NY, r % NC, lax.axis_index("head")


def device(z, y, c, x):
    return (z * (NY * NC) + y * NC + c, x)


def rendezvous(peers):
    barrier = pltpu.get_barrier_semaphore()
    for peer in peers:
        pl.semaphore_signal(barrier, inc=1, device_id=peer, device_id_type=MESH)
    pl.semaphore_wait(barrier, len(peers))


def remote(src, dst, send, recv, peer):
    return pltpu.make_async_remote_copy(
        src_ref=src, dst_ref=dst, send_sem=send, recv_sem=recv, device_id=peer, device_id_type=MESH
    )


def attend_kernel(
    rows_ref, gain1_ref, gain2_ref, cols_ref, accepted_ref, freq_ref, table_ref, cache_hbm, qkv_hbm,
    out_hbm, resid_out, normed_out, table_out, kv_out,
    mine, every, cache, qkv, out_w, terms, total, got, mine2, reach_v, cos_v, sin_v,
    load, send, recv, send_t, recv_t, send2, recv2, send3, recv3,
):
    z, y, c, x = place()
    tree, width = rows_ref.shape
    peers = [(x + d) % NX for d in (1, 3, 2)]
    loads = [pltpu.make_async_copy(qkv_hbm, qkv, load.at[0])]
    for d in (0, 1, 3, 2):
        p = (x + d) % NX
        loads.append(pltpu.make_async_copy(cache_hbm.at[p], cache.at[p], load.at[2 + d]))
    loads.append(pltpu.make_async_copy(out_hbm, out_w, load.at[1]))
    for copy in loads:
        copy.start()
    own = rms_norm(rows_ref[...], gain1_ref[...])
    mine[...] = own
    rendezvous([device(z, y, c, p) for p in peers])
    outgoing = []
    for d in (1, 3, 2):
        peer = device(z, y, c, (x + d) % NX)
        outgoing.append(
            remote(mine, every.at[x], send.at[d - 1], recv.at[d - 1], peer)
        )
        outgoing.append(
            remote(table_ref, table_out.at[x], send_t.at[d - 1], recv_t.at[d - 1], peer)
        )
    for copy in outgoing[0::2] + outgoing[1::2]:
        copy.start()
    every[x] = own
    table_out[x] = table_ref[...]

    count = NX * tree
    row = lax.broadcasted_iota(jnp.int32, (count, count), 0)
    column = lax.broadcasted_iota(jnp.int32, (count, count), 1)
    parent = cols_ref[:, 0:1]
    base = row - row % tree
    linked = ((parent >= 0) & (base + parent == column)) | (row == column)
    reach = jnp.where(linked, 1.0, 0.0)
    for turn in range((tree - 1).bit_length()):
        near = reach.astype(jnp.bfloat16)
        reach = jnp.minimum(jnp.dot(near, near, preferred_element_type=jnp.float32), 1.0)
    depth = jnp.sum(reach, axis=-1, keepdims=True) - 1.0
    for r in range(NX):
        reach_v[r] = reach[r * tree : (r + 1) * tree, r * tree : (r + 1) * tree]
    position = cols_ref[:, 1:2].astype(jnp.float32) + depth
    angle = position * freq_ref[...]
    head_dim = freq_ref.shape[1]
    lane = lax.broadcasted_iota(jnp.int32, (count, head_dim), 1)
    cos_v[...] = jnp.cos(angle)
    sine = jnp.sin(angle)
    sin_v[...] = jnp.where(lane < head_dim // 2, -sine, sine)
    loads[0].wait()
    group = qkv.shape[1] // head_dim - 2
    scale = 1.0 / math.sqrt(head_dim)

    def step(s, carry):
        d = s + s // 2 - 2 * (s // 3)
        p = (x + d) % NX

        @pl.when(s > 0)
        def _():
            remote(
                mine, every.at[p], send.at[3 - d], recv.at[3 - d], device(z, y, c, p)
            ).wait_recv()

        part = pl.ds(pl.multiple_of(p * tree, tree), tree)
        projected = jnp.dot(every[p], qkv[...], preferred_element_type=jnp.float32)
        cosine, sine = cos_v[part], sin_v[part]

        def turned(v):
            return (v * cosine + pltpu.roll(v, head_dim // 2, 1) * sine).astype(jnp.bfloat16)

        query = jnp.concatenate(
            [turned(projected[:, h * head_dim : (h + 1) * head_dim]) for h in range(group)], axis=0
        )
        key_new = turned(projected[:, group * head_dim : (group + 1) * head_dim])
        value_new = projected[:, (group + 1) * head_dim :].astype(jnp.bfloat16)
        fresh = jnp.concatenate([key_new, value_new], axis=1)
        chosen = accepted_ref[p] == lax.broadcasted_iota(
            jnp.int32, (accepted_ref.shape[1], tree), 1
        )
        kv_out[p, 0] = jnp.dot(
            jnp.where(chosen, 1.0, 0.0).astype(jnp.bfloat16), fresh,
            preferred_element_type=jnp.float32,
        ).astype(jnp.bfloat16)

        pltpu.make_async_copy(cache_hbm.at[p], cache.at[p], load.at[2 + d]).wait()
        nt = (((1,), (1,)), ((), ()))
        slots = cache.shape[1]
        length = cols_ref[pl.ds(pl.multiple_of(p * tree, tree), 1), 1:2]
        visible = lax.broadcasted_iota(jnp.int32, (1, slots), 1) < length
        old = lax.dot_general(
            query, cache[p, :, :head_dim], nt, preferred_element_type=jnp.float32
        ) * scale
        new = lax.dot_general(query, key_new, nt, preferred_element_type=jnp.float32) * scale
        old = jnp.where(visible, old, -1e30)
        seen = jnp.concatenate([reach_v[p]] * group, axis=0)
        new = jnp.where(seen > 0.5, new, -1e30)
        peak = jnp.maximum(
            jnp.max(old, axis=-1, keepdims=True), jnp.max(new, axis=-1, keepdims=True)
        )
        old = jnp.exp(old - peak)
        new = jnp.exp(new - peak)
        inverse = 1.0 / (
            jnp.sum(old, axis=-1, keepdims=True) + jnp.sum(new, axis=-1, keepdims=True)
        )
        mixed = jnp.dot(
            (old * inverse).astype(jnp.bfloat16), cache[p, :, head_dim:],
            preferred_element_type=jnp.float32,
        ) + jnp.dot(
            (new * inverse).astype(jnp.bfloat16), value_new, preferred_element_type=jnp.float32
        )
        mixed = mixed.astype(jnp.bfloat16)
        mixed = jnp.concatenate([mixed[h * tree : (h + 1) * tree] for h in range(group)], axis=1)

        @pl.when(s == 0)
        def _():
            loads[-1].wait()

        term = jnp.dot(mixed, out_w[...], preferred_element_type=jnp.float32)

        @pl.when(s == 0)
        def _():
            total[...] = term + rows_ref[...].astype(jnp.float32)

        @pl.when(s > 0)
        def _():
            terms[d - 1] = term.astype(jnp.bfloat16)
            remote(
                terms.at[d - 1], got.at[d - 1], send2.at[d - 1], recv2.at[d - 1],
                device(z, y, c, p),
            ).start()

        return carry

    lax.fori_loop(0, NX, step, 0)
    returns = [
        remote(
            terms.at[d - 1], got.at[d - 1], send2.at[d - 1], recv2.at[d - 1],
            device(z, y, c, (x + d) % NX),
        )
        for d in (1, 3, 2)
    ]
    for copy in returns:
        copy.wait_recv()
    resid = total[...]
    for i in range(3):
        resid = resid + got[i].astype(jnp.float32)
    resid = resid.astype(jnp.bfloat16)
    resid_out[...] = resid
    normed = rms_norm(resid, gain2_ref[...])
    mine2[...] = normed
    last = [
        remote(mine2, normed_out.at[x], send3.at[d - 1], recv3.at[d - 1], device(z, y, c, (x + d) % NX))
        for d in (1, 3, 2)
    ]
    for copy in last:
        copy.start()
    normed_out[x] = normed
    for copy in returns + outgoing[0::2]:
        copy.wait_send()
    for copy in outgoing[1::2] + last:
        copy.wait()


def attend(rows, gain1, gain2, parents, lengths, accepted, table, cache, w_qkv, w_out):
    tree, width = rows.shape
    slots, pair = cache.shape[-2:]
    head_dim = pair // 2
    half = head_dim // 2
    frequency = ROPE_BASE ** (-jnp.arange(half, dtype=jnp.float32) / half)
    frequency = jnp.concatenate([frequency, frequency])[None]
    lengths = jnp.broadcast_to(lengths[:, None], parents.shape)
    cols = jnp.stack([parents.reshape(-1), lengths.reshape(-1)], axis=1)
    bf16 = jnp.bfloat16
    sem = pltpu.SemaphoreType.DMA((3,))
    hbm = pl.BlockSpec(memory_space=pl.ANY)
    return pl.pallas_call(
        attend_kernel,
        out_shape=(
            jax.ShapeDtypeStruct((tree, width), bf16),
            jax.ShapeDtypeStruct((NX, tree, width), bf16),
            jax.ShapeDtypeStruct((NX,) + table.shape, table.dtype),
            jax.ShapeDtypeStruct((NX, 1, accepted.shape[1], pair), bf16),
        ),
        in_specs=[VMEM] * 7 + [hbm] * 3,
        out_specs=(VMEM,) * 4,
        scratch_shapes=[
            pltpu.VMEM((tree, width), bf16),
            pltpu.VMEM((NX, tree, width), bf16),
            pltpu.VMEM((NX, slots, pair), bf16),
            pltpu.VMEM(w_qkv.shape, bf16),
            pltpu.VMEM(w_out.shape, bf16),
            pltpu.VMEM((3, tree, width), bf16),
            pltpu.VMEM((tree, width), jnp.float32),
            pltpu.VMEM((3, tree, width), bf16),
            pltpu.VMEM((tree, width), bf16),
            pltpu.VMEM((NX, tree, tree), jnp.float32),
            pltpu.VMEM((NX * tree, head_dim), jnp.float32),
            pltpu.VMEM((NX * tree, head_dim), jnp.float32),
            pltpu.SemaphoreType.DMA((6,)),
        ] + [sem] * 8,
        compiler_params=pltpu.CompilerParams(collective_id=1, has_side_effects=True),
        name="attend",
    )(
        rows, gain1[None], gain2[None], cols, accepted[:, :, None], frequency, table,
        cache.reshape(NX, slots, pair), w_qkv, w_out,
    )


def exchange_kernel(src, out, mid_y, mid_z, send1, recv1, send2, recv2, local):
    z, y, c, x = place()
    half = src.shape[-1] // 2
    left, right = pl.ds(0, half), pl.ds(half, half)
    order = (1, 3, 2)
    peers = [device(z, (y + d) % NY, (c + e) % NC, x) for d in order for e in range(NC)]
    peers += [device((z + d) % NZ, y, (c + e) % NC, x) for d in order for e in range(NC)]
    peers += [device(z, y, 1 - c, x)]
    rendezvous(peers)
    copies = []
    arrive_y, arrive_z = {}, {}
    for d in order:
        yd, zd = (y + d) % NY, (z + d) % NZ
        copy = remote(
            src.at[:, yd, :, :, left], mid_y.at[d - 1], send1.at[0, d - 1], recv1.at[0, d - 1],
            device(z, yd, c, x),
        )
        copy.start()
        arrive_y[d] = copy
        copy = remote(
            src.at[zd, :, :, :, right], mid_z.at[d - 1], send1.at[1, d - 1], recv1.at[1, d - 1],
            device(zd, y, c, x),
        )
        copy.start()
        arrive_z[d] = copy

    for d in (0,) + order:
        ys, zs = (y - d) % NY, (z - d) % NZ
        if d:
            arrive_y[d].wait_recv()
            arrive_z[d].wait_recv()
        for f in order + (0,):
            yf, zf = (y + f) % NY, (z + f) % NZ
            for e in range(NC):
                ce = (c + e) % NC
                slot = (d * 4 + f) * NC + e
                a = src.at[zf, y, ce, :, left] if d == 0 else mid_y.at[d - 1, zf, ce]
                b = src.at[z, yf, ce, :, right] if d == 0 else mid_z.at[d - 1, yf, ce]
                to_a, to_b = out.at[z, ys, c, :, left], out.at[zs, y, c, :, right]
                if f == 0 and e == 0:
                    pair = [
                        pltpu.make_async_copy(a, to_a, local.at[0, d]),
                        pltpu.make_async_copy(b, to_b, local.at[1, d]),
                    ]
                else:
                    pair = [
                        remote(a, to_a, send2.at[0, slot], recv2.at[0, slot], device(zf, y, ce, x)),
                        remote(b, to_b, send2.at[1, slot], recv2.at[1, slot], device(z, yf, ce, x)),
                    ]
                for copy in pair:
                    copy.start()
                copies += pair
    for d in order:
        arrive_y[d].wait_send()
        arrive_z[d].wait_send()
    for copy in copies:
        copy.wait()


def exchange(blocks, identifier):
    rows, width = blocks.shape[-2:]
    return pl.pallas_call(
        exchange_kernel,
        out_shape=jax.ShapeDtypeStruct(blocks.shape, blocks.dtype),
        in_specs=[VMEM],
        out_specs=VMEM,
        scratch_shapes=[
            pltpu.VMEM((3, NZ, NC, rows, width // 2), blocks.dtype),
            pltpu.VMEM((3, NY, NC, rows, width // 2), blocks.dtype),
            pltpu.SemaphoreType.DMA((2, 3)),
            pltpu.SemaphoreType.DMA((2, 3)),
            pltpu.SemaphoreType.DMA((2, 32)),
            pltpu.SemaphoreType.DMA((2, 32)),
            pltpu.SemaphoreType.DMA((2, 4)),
        ],
        compiler_params=pltpu.CompilerParams(collective_id=identifier, has_side_effects=True),
        name="exchange",
    )(blocks)


def final_kernel(part_ref, own_ref, live_ref, out, got, send, recv):
    z, y, c, x = place()
    peers = [(x + d) % NX for d in (1, 3, 2)]
    rendezvous([device(z, y, c, p) for p in peers])
    copies = [
        remote(part_ref.at[p], got.at[i], send.at[i], recv.at[i], device(z, y, c, p))
        for i, p in enumerate(peers)
    ]
    for copy in copies:
        copy.start()
    for copy in copies:
        copy.wait()
    total = own_ref[...]
    for i in range(3):
        total = total + got[i].astype(jnp.float32)
    out[...] = jnp.where(live_ref[...] == 1, total, 0.0).astype(jnp.bfloat16)


def final_rows(part, own, live):
    rows, width = own.shape
    return pl.pallas_call(
        final_kernel,
        out_shape=jax.ShapeDtypeStruct((rows, width), jnp.bfloat16),
        in_specs=[VMEM] * 3,
        out_specs=VMEM,
        scratch_shapes=[
            pltpu.VMEM((3, rows, width), jnp.bfloat16),
            pltpu.SemaphoreType.DMA((3,)),
            pltpu.SemaphoreType.DMA((3,)),
        ],
        compiler_params=pltpu.CompilerParams(collective_id=5, has_side_effects=True),
        name="final_rows",
    )(part, own, live)


def expert_half(rows, inner, outer):
    both = jnp.dot(rows, inner, preferred_element_type=jnp.float32)
    half = inner.shape[1] // 2
    hidden = (jax.nn.silu(both[:, :half]) * both[:, half:]).astype(jnp.bfloat16)
    return jnp.dot(hidden, outer, preferred_element_type=jnp.float32).astype(jnp.bfloat16)


def body(
    tokens,
    live,
    parents,
    lengths,
    accepted,
    routes,
    cache,
    attn_gain,
    w_qkv,
    w_out,
    ffn_gain,
    shared_gate,
    shared_up,
    shared_down,
    router,
    expert_in,
    expert_out,
):
    tree, width = tokens.shape[1:]
    own_rows = tokens[0]
    x = lax.axis_index("head")
    top_count = routes.shape[2]
    expert_count = router.shape[1]
    capacity = 4 * tree * top_count // (3 * expert_count)

    table = jnp.pad(routes[0].T, ((0, 8 - top_count), (0, 128 - tree)))
    resid, normed2, table_all, accepted_kv = attend(
        own_rows, attn_gain, ffn_gain, parents, lengths, accepted, table, cache, w_qkv, w_out
    )
    normed2 = normed2.reshape(NX * tree, width)

    choose = table_all[:, :top_count, :tree]
    named = jnp.any(
        choose[:, :, :, None] == jnp.arange(expert_count, dtype=jnp.int32), axis=1
    ).astype(jnp.float32)
    earlier = jnp.tril(jnp.ones((tree, tree), jnp.bfloat16), -1)
    rank = jnp.einsum(
        "ts,rse->rte", earlier, named.astype(jnp.bfloat16), preferred_element_type=jnp.float32
    )
    logits = jnp.dot(normed2, router, preferred_element_type=jnp.float32)
    picked = jax.nn.sigmoid(logits).reshape(NX, tree, expert_count) * named
    gates = picked / jnp.sum(picked, axis=-1, keepdims=True)
    pair = x // 2
    slot = jnp.where(named > 0.5, rank, -1.0)

    def of_pair(values):
        values = values.reshape(NX, tree, GROUP, expert_count // GROUP)
        return jnp.where(pair == 0, values[..., 0], values[..., 1])

    slot = of_pair(slot)
    gates = of_pair(gates)
    same = jnp.arange(NX)[:, None, None, None, None] == jnp.arange(NX)[:, None]
    taken = (slot[:, :, :, None, None] == jnp.arange(capacity, dtype=jnp.float32)) & same
    taken = taken.reshape(NX * tree, GROUP * NX * capacity)
    weight = jnp.broadcast_to(
        gates[:, :, :, None, None], (NX, tree, GROUP, NX, capacity)
    ).reshape(NX * tree, GROUP * NX * capacity)
    weight = jnp.where(taken, weight, 0.0)
    weight_high = weight.astype(jnp.bfloat16)
    weight_low = (weight - weight_high.astype(jnp.float32)).astype(jnp.bfloat16)
    outgoing = lax.dot_general(
        taken.astype(jnp.bfloat16), normed2, (((0,), (0,)), ((), ())),
        preferred_element_type=jnp.float32,
    ).astype(jnp.bfloat16)
    blocks = (NZ, NY, NC, NX * capacity, width)
    received = exchange(outgoing.reshape(blocks), 3)
    half_out = expert_half(received.reshape(-1, width), expert_in[0], expert_out[0])
    returned = exchange(half_out.reshape(blocks), 4).reshape(-1, width)

    gated = jax.nn.silu(jnp.dot(normed2, shared_gate, preferred_element_type=jnp.float32))
    hidden = (gated * jnp.dot(normed2, shared_up, preferred_element_type=jnp.float32)).astype(
        jnp.bfloat16
    )
    part = (
        jnp.dot(hidden, shared_down, preferred_element_type=jnp.float32)
        + jnp.dot(weight_high, returned, preferred_element_type=jnp.float32)
        + jnp.dot(weight_low, returned, preferred_element_type=jnp.float32)
    ).reshape(NX, tree, width)
    own_part = lax.dynamic_index_in_dim(part, x, 0, keepdims=False) + resid.astype(jnp.float32)
    hidden_out = final_rows(part.astype(jnp.bfloat16), own_part, live.reshape(tree, 1))
    return (hidden_out[None], accepted_kv)


def solution(mesh):
    in_specs = (
        P(("req", "head"), None, None),
        P(("req", "head"), None),
        P("req", None),
        P("req"),
        P("req", None),
        P(("req", "head"), None, None),
        P("req", "head", None, None),
        P(),
        P(None, "head"),
        P("head", None),
        P(),
        P(None, "head"),
        P(None, "head"),
        P("head", None),
        P(),
        P(("req", "head"), None, None),
        P(("req", "head"), None, None),
    )
    out_specs = (P(("req", "head"), None, None), P("req", "head", None, None))
    return jax.shard_map(body, mesh=mesh, in_specs=in_specs, out_specs=out_specs, check_vma=False)
```
